32 devices in a mesh: sector: 4 (over y, x), rev: 8 (over z, core).
Axes of the slice: x: 2, y: 2, z: 4, core: 2. Of those that a mesh axis runs over, the one named last changes fastest.
Arguments:
- ranges: float32 [128, 2048, 128], P('rev', 'sector'), may hold values from 0.9 to 13
- valid_mask: int32 [128, 2048, 128], P('rev', 'sector'), may hold values 0 or 1
- match_tile: int32 [128, 2048], P('rev', 'sector'), may hold values from 0 to 4095
- map_points: float32 [4096, 3, 128], replicated, may hold values from -5 to 5
- revolution_knot: int32 [128], P('rev'), may hold values from 0 to 124
- spline_points: float32 [128, 3], replicated, may hold values from -4 to 4
- prior_weights: float32 [768], replicated, may hold values from 0.3 to 3
Outputs:
- surface_normals: float32 [3, 128, 2048, 128], P(None, 'rev', 'sector')
- knot_update: float32 [768], replicated
The draws below stay inside these ranges and needn't reach their ends.
All inputs are finite; a program needn't handle non-finite values. No bound on the sum of `valid_mask` on one device may be relied on, other than what follows from the above.
Results may differ from the reference program's by a relative error of at most 0.0003.
Values sent between devices are 32-bit elements; how exact they have to be, the bound alone decides.
No kernel may reach another device: no remote copies, remote signals or barrier semaphores. Data moves between devices by JAX's collectives and lax.ppermute only.
A program may use at most 256 MiB of HBM per device.

```python
import math
import jax
import jax.numpy as jnp
from jax import lax

BEAMS = 128
COLS = 2048
KNOTS = 128
MAPN = 4096
REVS = 128
UNK = 768


def draw_ranges(key, part):
    column = jnp.arange(COLS, dtype=jnp.int32).astype(jnp.float32)[None, :, None]
    level = 2.0 + 4.0 * column / COLS
    noise = jnp.exp(0.25 * jnp.clip(jax.random.normal(key, (REVS, COLS, BEAMS), jnp.float32), -3.0, 3.0))
    return level * noise


def draw_revolution_knot(key, part):
    revolution = jnp.arange(REVS, dtype=jnp.int32)
    base_knot = revolution * (KNOTS - 4) // max(REVS - 1, 1)
    jitter = jax.random.randint(key, (REVS,), -1, 2, dtype=jnp.int32)
    inner = (revolution > 0) & (revolution < REVS - 1)
    return jnp.clip(base_knot + jnp.where(inner, jitter, 0), 0, KNOTS - 4).astype(jnp.int32)


def with_ends(values, own_key, smallest, top_value):
    longest = values.shape.index(max(values.shape))
    spots = []
    for shift in (0, 1):
        where = [jax.random.randint(jax.random.fold_in(own_key, axis), (), 0, length) for axis, length in enumerate(values.shape)]
        where[longest] = (where[longest] + shift) % values.shape[longest]
        spots.append(tuple(where))
    return values.at[spots[0]].set(smallest).at[spots[1]].set(top_value)


def scatter_about(own_key, extent, scale, bound, kind=jnp.bfloat16):
    return jnp.clip(scale * jax.random.normal(own_key, extent, jnp.float32), -bound, bound).astype(kind)


def setup_inputs(seed: int = 0) -> dict:
    streams_of = jax.random.split(jax.random.key(seed), 8)
    return {
        "ranges": draw_ranges(jax.random.fold_in(streams_of[7], 71), 0),
        "valid_mask": with_ends((jax.random.randint(streams_of[1], (REVS, COLS, BEAMS), 0, 10) < 9).astype(jnp.int32), jax.random.fold_in(streams_of[1], 1), 0, 1),
        "match_tile": with_ends(jax.random.randint(streams_of[2], (REVS, COLS), 0, MAPN), jax.random.fold_in(streams_of[2], 1), 0, MAPN - 1).astype(jnp.int32),
        "map_points": scatter_about(streams_of[3], (MAPN, 3, BEAMS), 1.0, 5.0, jnp.float32),
        "revolution_knot": draw_revolution_knot(jax.random.fold_in(streams_of[7], 71), 0),
        "spline_points": scatter_about(streams_of[5], (KNOTS, 3), 1.0, 4.0, jnp.float32),
        "prior_weights": jnp.clip(jnp.exp(jax.random.uniform(streams_of[6], (UNK,), jnp.float32, math.log(0.3), math.log(3.0))), 0.3, 3.0),
    }


HIGHEST = lax.Precision.HIGHEST

def basis_weights(column_phase):
    phase_square = column_phase * column_phase
    phase_cube = phase_square * column_phase
    return jnp.stack([(1.0 - column_phase) ** 3 / 6.0, (3.0 * phase_cube - 6.0 * phase_square + 4.0) / 6.0, (-3.0 * phase_cube + 3.0 * phase_square + 3.0 * column_phase + 1.0) / 6.0, phase_cube / 6.0])

def unit_directions(column):
    beam_index = jnp.arange(BEAMS, dtype=jnp.int32).astype(jnp.float32)
    elevation = -0.4 + 0.7 * beam_index / (BEAMS - 1)
    azimuth = 2.0 * jnp.pi * column / COLS
    return jnp.stack([jnp.cos(elevation)[None, :] * jnp.cos(azimuth)[:, None], jnp.cos(elevation)[None, :] * jnp.sin(azimuth)[:, None], jnp.broadcast_to(jnp.sin(elevation)[None, :], (column.shape[0], BEAMS))])

def cross_product(former, latter):
    return jnp.stack([former[1] * latter[2] - former[2] * latter[1], former[2] * latter[0] - former[0] * latter[2], former[0] * latter[1] - former[1] * latter[0]])

def reference(ranges, valid_mask, match_tile, map_points, revolution_knot, spline_points, prior_weights):
    column = jnp.arange(COLS, dtype=jnp.int32).astype(jnp.float32)
    weights = basis_weights(column / COLS)
    unit_rays = unit_directions(column)
    basis_pair = weights[:, None, :] * weights[None, :, :]
    per_point = 1.0 / (COLS * BEAMS)

    def one_revolution(pieces):
        range_row, live_row, match_row, knot_row = pieces
        control = lax.dynamic_slice(spline_points, (knot_row, jnp.int32(0)), (4, 3))
        offset = weights[0][None, :] * control[0][:, None] + weights[1][None, :] * control[1][:, None] + weights[2][None, :] * control[2][:, None] + weights[3][None, :] * control[3][:, None]
        points = range_row[None] * unit_rays + offset[:, :, None]
        along_cols = jnp.roll(points, -1, axis=1) - jnp.roll(points, 1, axis=1)
        edge_padded = jnp.concatenate([points[..., :1], points, points[..., -1:]], axis=2)
        along_beams = edge_padded[..., 2:] - edge_padded[..., :-2]
        crossed = cross_product(along_beams, along_cols)
        normals = crossed / jnp.sqrt(lax.optimization_barrier(jnp.sum(crossed * crossed, axis=0)) + 1.0)
        targets = jnp.transpose(map_points[match_row], (1, 0, 2))
        residual = lax.optimization_barrier(jnp.sum(normals * (points - targets), axis=0))
        live_mask = live_row.astype(jnp.float32)
        spread = jnp.sum(live_mask * residual * residual) / jnp.maximum(jnp.sum(live_mask), 1.0) + 1e-06
        robust = live_mask / (1.0 + residual * residual / spread)
        jacobian = jnp.concatenate([cross_product(points, normals), normals], axis=0)
        weighted = jacobian * robust[None]
        column_gram = jnp.einsum('acx,ecx->aec', weighted, jacobian, precision=HIGHEST)
        column_grad = jnp.einsum('acx,cx->ac', weighted, residual, precision=HIGHEST)
        gram = jnp.einsum('jic,aec->jaie', basis_pair, column_gram, precision=HIGHEST) * per_point
        grad = jnp.einsum('jc,ac->ja', weights, column_grad, precision=HIGHEST) * per_point
        return (normals, gram, grad)
    normals, gram, grad = lax.map(one_revolution, (ranges, valid_mask, match_tile, revolution_knot))

    def place_block(carry, pieces):
        matrix, vector = carry
        block, part, knot_row = pieces
        start = (6 * knot_row).astype(jnp.int32)
        corner = lax.dynamic_slice(matrix, (start, start), (24, 24))
        matrix = lax.dynamic_update_slice(matrix, corner + block.reshape(24, 24), (start, start))
        segment = lax.dynamic_slice(vector, (start,), (24,))
        vector = lax.dynamic_update_slice(vector, segment + part.reshape(24), (start,))
        return ((matrix, vector), None)
    start_state = (jnp.zeros((UNK, UNK), jnp.float32), jnp.zeros((UNK,), jnp.float32))
    (matrix, vector), _ = lax.scan(place_block, start_state, (gram, grad, revolution_knot))
    system = matrix + jnp.diag(prior_weights)
    factor = jnp.linalg.cholesky(system)
    update = -jax.scipy.linalg.cho_solve((factor, True), vector)
    return (jnp.transpose(normals, (1, 0, 2, 3)), update)
```

```python
import functools

import jax
import jax.numpy as jnp
import numpy as np
from jax import lax
from jax.experimental import pallas as pl
from jax.experimental.pallas import tpu as pltpu
from jax.sharding import PartitionSpec as P

COLS = 2048
PAD = 8
F32 = jnp.float32
BF16 = jnp.bfloat16
NPROD = 27
GRAD0 = 21
PAIRS = [(a, e) for a in range(6) for e in range(a, 6)]
PAIR_ID = {}
for _n, (_a, _e) in enumerate(PAIRS):
    PAIR_ID[_a, _e] = PAIR_ID[_e, _a] = _n
JPAIRS = [(j, i) for j in range(4) for i in range(j, 4)]
JPAIR_ID = {}
for _n, (_j, _i) in enumerate(JPAIRS):
    JPAIR_ID[_j, _i] = JPAIR_ID[_i, _j] = _n
NB = 24
GL = 64
LEFT = 104
KNOT_LANE = 27


def lane_iota(rows):
    return lax.broadcasted_iota(jnp.int32, (rows, 128), 1)


def points_kernel(
    first_ref, knot_ref, spline_ref, match_ref,
    range_ref, mask_ref, left_ref, right_ref, map_ref, trig_ref, beam_ref,
    normal_ref, resid_ref, sums_ref, pts,
    tiles, stage0, stage1,
    *, width, mapn, revs,
):
    r = pl.program_id(0)
    cosb = beam_ref[0:1, :]
    sinb = beam_ref[1:2, :]

    @pl.when(r == 0)
    def _():
        sums_ref[...] = jnp.zeros_like(sums_ref)

        def tile_body(t, carry):
            start = pl.multiple_of(t * 8, 8)
            for d in range(3):
                tiles[pl.ds(start * 4 + d, 8, stride=4), :] = map_ref[d, pl.ds(start, 8), :]
            return carry

        lax.fori_loop(0, mapn // 8, tile_body, 0, unroll=4)

    knot = knot_ref[r]
    cubic = []
    for d in range(3):
        c = [spline_ref[d, knot + j] for j in range(4)]
        cubic.append(
            (
                (c[0] + 4.0 * c[1] + c[2]) * (1.0 / 6.0),
                (c[2] - c[0]) * 0.5,
                (c[0] - 2.0 * c[1] + c[2]) * 0.5,
                (c[3] - c[0] + 3.0 * (c[1] - c[2])) * (1.0 / 6.0),
            )
        )
    first = first_ref[0]
    row_iota = lax.broadcasted_iota(jnp.int32, (8, 128), 0)

    def put_points(start, rng, column):
        u = (row_iota + column).astype(F32) * (1.0 / COLS)
        offset = [((k[3] * u + k[2]) * u + k[1]) * u + k[0] for k in cubic]
        rows = pl.ds(start, 8)
        flat = rng * cosb
        pts[0, 0, rows, :] = flat * trig_ref[0, rows, :] + offset[0]
        pts[1, 0, rows, :] = flat * trig_ref[1, rows, :] + offset[1]
        pts[2, 0, rows, :] = rng * sinb + offset[2]

    put_points(
        0, jnp.broadcast_to(left_ref[0], (8, 128)), jnp.where(first == 0, COLS, first) - PAD
    )
    put_points(
        width + PAD,
        jnp.broadcast_to(right_ref[0], (8, 128)),
        jnp.where(first + width == COLS, 0, first + width),
    )

    def point_body(t, carry):
        for n in range(16):
            start = pl.multiple_of(t * 128 + 8 * n, 8)
            put_points(start + PAD, range_ref[0, pl.ds(start, 8), :], first + start)
        return carry

    lax.fori_loop(0, width // 128, point_body, 0)

    lanes = lane_iota(8)
    first_lane = lanes == 0
    last_lane = lanes == 127
    cup, cdn = (beam_ref[2:3, :], beam_ref[3:4, :])
    sup, sdn = (beam_ref[4:5, :], beam_ref[5:6, :])

    def gather(base, stage):
        here = r * width + base
        for c in range(64):
            row = pl.multiple_of(match_ref[here + c], 4)
            stage[pl.ds(4 * c, 4), :] = tiles[pl.ds(row, 4), :]

    def compute(base, stage, acc):
        sq, cnt = acc
        for s in range(8):
            start = base + 8 * s
            rng = range_ref[0, pl.ds(start, 8), :]
            up = jnp.where(last_lane, rng, pltpu.roll(rng, 127, 1))
            dn = jnp.where(first_lane, rng, pltpu.roll(rng, 1, 1))
            q = up * cup - dn * cdn
            bz = up * sup - dn * sdn
            bx = q * trig_ref[0, pl.ds(start + PAD, 8), :]
            by = q * trig_ref[1, pl.ds(start + PAD, 8), :]
            dx, dy, dz = (
                pts[d, 0, pl.ds(start + PAD + 1, 8), :] - pts[d, 0, pl.ds(start + PAD - 1, 8), :]
                for d in range(3)
            )
            cx = by * dz - bz * dy
            cy = bz * dx - bx * dz
            cz = bx * dy - by * dx
            inv = lax.rsqrt(cx * cx + cy * cy + cz * cz + 1.0)
            n = (cx * inv, cy * inv, cz * inv)
            res = jnp.zeros((8, 128), F32)
            for d in range(3):
                normal_ref[d, 0, pl.ds(start, 8), :] = n[d]
                target = stage[pl.ds(32 * s + d, 8, stride=4), :]
                res = res + n[d] * (pts[d, 0, pl.ds(start + PAD, 8), :] - target)
            resid_ref[0, pl.ds(start, 8), :] = res
            live = mask_ref[0, pl.ds(start, 8), :].astype(F32)
            sq = sq + live * res * res
            cnt = cnt + live
        return (sq, cnt)

    gather(0, stage0)
    pairs = width // 128

    def chunk_body(t, acc):
        base = pl.multiple_of(t * 128, 128)
        gather(base + 64, stage1)
        acc = compute(base, stage0, acc)
        gather(jnp.where(t + 1 < pairs, base + 128, 0), stage0)
        return compute(base + 64, stage1, acc)

    zero = jnp.zeros((8, 128), F32)
    sq, cnt = lax.fori_loop(0, pairs, chunk_body, (zero, zero))
    here = lane_iota(1) == r
    sums_ref[0:1, :] = jnp.where(here, jnp.sum(sq), sums_ref[0:1, :])
    sums_ref[1:2, :] = jnp.where(here, jnp.sum(cnt), sums_ref[1:2, :])


def gram_kernel(
    knot_ref,
    point_ref, mask_ref, resid_ref, normal_ref, sums_ref, basis_ref,
    mix_ref, out_ref,
    even, odd, grads,
    *, width, scale, revs,
):
    step = pl.program_id(0)
    square, count = (sums_ref[0:1, :], sums_ref[1:2, :])
    inv_all = 1.0 / (square / jnp.maximum(count, 1.0) + 1e-06)
    lanes = lane_iota(16)
    row_lanes = lane_iota(1)

    def products(h, inv_spread, start, prods, sums):
        sums = list(sums)
        rows = pl.ds(start, 16)
        rows_pad = pl.ds(pl.multiple_of(start + PAD, 8), 16)
        px, py, pz = (point_ref[d, h, rows_pad, :] for d in range(3))
        nx, ny, nz = (normal_ref[d, h, rows, :] for d in range(3))
        res = resid_ref[h, rows, :]
        live = mask_ref[h, rows, :].astype(F32)
        robust = live / (1.0 + res * res * inv_spread)
        jac = (py * nz - pz * ny, pz * nx - px * nz, px * ny - py * nx, nx, ny, nz)
        wjac = [robust * j for j in jac]
        for n, (a, e) in enumerate(PAIRS):
            prods[n, rows, :] = (wjac[a] * jac[e]).astype(BF16)
        weighted = robust * res
        for part in range(2):
            span = slice(8 * part, 8 * part + 8)
            for a in range(6):
                total = jac[a][span] * weighted[span]
                for level in range(4):
                    total = sums[4 * a + level] + total
                    sums[4 * a + level] = total
        return sums

    def contract(k, prods, table):
        pair = jnp.concatenate([prods[2 * k], prods[2 * k + 1]], axis=1)
        part = jnp.dot(basis_ref[...], pair, preferred_element_type=F32)
        part = part[0:16, :] + part[16:32, :]
        for n in range(2):
            total = jnp.sum(part[:, 128 * n:128 * (n + 1)], axis=1, keepdims=True)
            table = jnp.where(lanes == 2 * k + n, total, table)
        return table

    def finish(rev, table, grads):
        table = table * scale
        grads = grads * scale
        out = []
        for j in range(4):
            line = jnp.where(row_lanes == KNOT_LANE, knot_ref[rev], grads[j:j + 1, :])
            for i in range(4):
                piece = table[JPAIR_ID[j, i]:JPAIR_ID[j, i] + 1, :]
                piece = jnp.where(row_lanes < GRAD0, piece, 0.0)
                if i:
                    piece = pltpu.roll(piece, 32 * i, 1)
                line = line + piece
            out.append(line)
        out_ref[pl.ds(pl.multiple_of(rev * 4, 4), 4), :] = jnp.concatenate(out, axis=0)

    trips = 4
    items = width // 32 // trips
    empty = jnp.zeros((16, 128), F32)
    pairs = (GRAD0 + 1) // 2
    each = -(-pairs // trips)

    def gradient(sums):
        out = jnp.zeros((8, 128), F32)
        for j in range(4):
            total = jnp.zeros((1, 128), F32)
            for a in range(6):
                value = jnp.zeros((8, 128), F32)
                for level in range(4):
                    value = value + mix_ref[4 * j + level] * sums[4 * a + level]
                total = jnp.where(row_lanes == GRAD0 + a, jnp.sum(value), total)
            out = jnp.where(lane_rows == j, total, out)
        return out

    lane_rows = lax.broadcasted_iota(jnp.int32, (8, 128), 0)
    for h in range(2):
        now, done = (even, odd) if h == 0 else (odd, even)
        r = 2 * step + h
        inv_spread = jnp.sum(jnp.where(row_lanes == r, inv_all, 0.0), axis=1, keepdims=True)
        inv_spread = jnp.broadcast_to(inv_spread, (16, 128))

        def body(t, carry, h=h, now=now, done=done, inv_spread=inv_spread):
            table, sums = (carry[0], carry[1:])
            for u in range(max(each, items)):
                if u < each:
                    table = contract(jnp.minimum(t * each + u, pairs - 1), done, table)
                if u < items:
                    for part in range(2):
                        start = pl.multiple_of((t * items + u) * 32 + 16 * part, 16)
                        sums = products(h, inv_spread, start, now, sums)
            return (table, *sums)

        zero = jnp.zeros((8, 128), F32)
        table, *sums = lax.fori_loop(0, trips, body, (empty,) + (zero,) * 24)
        finish(jnp.maximum(r - 1, 0), table, grads[...])
        grads[...] = gradient(sums)

    @pl.when(step == revs // 2 - 1)
    def _():
        table = lax.fori_loop(0, pairs, lambda k, t: contract(k, odd, t), empty, unroll=True)
        finish(revs - 1, table, grads[...])


def placement():
    mats = []
    index = {}
    for a in range(6):
        for s in range(4):
            for wrap in range(2 if s else 1):
                m = np.zeros((128, 128), np.float32)
                for i in range(4):
                    for e in range(6):
                        lane = 6 * (i + s) + e - NB * wrap
                        m[32 * i + PAIR_ID[a, e], lane % 128] = 1.0
                m[GRAD0 + a, GL] = 1.0
                index[a, s, wrap] = len(mats)
                mats.append(m)
    return np.stack(mats), index


PLACE, PLACE_ID = placement()


def split3(x):
    a = x.astype(BF16)
    b = x - a.astype(F32)
    m = b.astype(BF16)
    return (a, m, (b - m.astype(F32)).astype(BF16))


def solve_kernel(own_ref, *refs, blocks, revs, sources):
    shares = refs[:sources]
    prior_ref, place_ref, out_ref, x_ref, front, sol = refs[sources:]
    each = 2 * revs // sources
    for k in range(sources):
        for side in range(2):
            src = own_ref[0] ^ (2 * k + side)
            x_ref[pl.ds(pl.multiple_of(src * each, 8), each), :] = shares[k][
                side * each:(side + 1) * each, :
            ]
    stride = blocks + 8
    knots = 4 * blocks
    lanes_b = lane_iota(blocks)

    knot_col = x_ref[pl.ds(0, revs, stride=4), :][:, KNOT_LANE:KNOT_LANE + 1]
    knot_col = jnp.broadcast_to((knot_col + 0.5).astype(jnp.int32), (revs, knots))
    slot = lax.broadcasted_iota(jnp.int32, (revs, knots), 1)
    s_of = slot // blocks
    m_of = slot - s_of * blocks
    dims = (((0,), (0,)), ((), ()))
    sums = {}
    for shift in range(2):
        hot = jnp.where(knot_col == 4 * (m_of - shift) + s_of, 1.0, 0.0).astype(BF16)
        for j in range(4):
            parts = split3(x_ref[pl.ds(j, revs, stride=4), :])
            total = None
            for part in parts:
                y = lax.dot_general(hot, part, dims, preferred_element_type=F32)
                total = y if total is None else total + y
            sums[shift, j] = split3(total)

    rows = {}
    for a in range(6):
        for s in range(4):
            for wrap in range(2 if s else 1):
                js = range(4 - s, 4) if wrap else range(4 - s)
                lhs = jnp.concatenate(
                    [sums[wrap, j][k][s * blocks:(s + 1) * blocks] for k in range(3) for j in js],
                    axis=0,
                )
                y = jnp.dot(lhs, place_ref[PLACE_ID[a, s, wrap]], preferred_element_type=F32)
                count = len(js) * blocks
                y = y[0:count] + y[count:2 * count] + y[2 * count:3 * count]
                for n, j in enumerate(js):
                    q = 6 * ((s + j) % 4) + a
                    part = y[n * blocks:(n + 1) * blocks]
                    rows[q] = part if q not in rows else rows[q] + part
    prior = prior_ref[...]
    for q in range(NB):
        front[q * stride:q * stride + blocks, :] = rows[q] + jnp.where(lanes_b == q, prior, 0.0)

    def column(x, k):
        return jnp.broadcast_to(x[:, k:k + 1], x.shape)

    def eliminate(mat):
        for k in range(NB):
            pivot = mat[k] / column(mat[k], k)
            mat = [pivot if q == k else mat[q] - column(mat[q], k) * pivot for q in range(NB)]
        return mat

    sol[...] = jnp.zeros_like(sol)
    levels = []
    step = 1
    n = blocks // 2
    lanes = lane_iota(NB)
    near = (lanes < NB) | (lanes == GL)
    zeros = jnp.zeros((NB, 128), F32)
    while n >= 1:
        odd = eliminate([front[pl.ds(q * stride + step, n, stride=2 * step), :] for q in range(NB)])
        for q in range(NB):
            front[pl.ds(q * stride + step, n, stride=2 * step), :] = odd[q]
        plus = zeros
        for i in range(n):
            x = front[pl.ds((2 * i + 1) * step, NB, stride=stride), :]
            right = jnp.where((lanes >= NB) & (lanes < 2 * NB), x, 0.0)
            left = jnp.where(lanes >= LEFT, x, 0.0)
            rhs = jnp.where(lanes == GL, x, 0.0)
            minus = rhs + right + pltpu.roll(left, NB, 1)
            mat = jnp.concatenate(
                [zeros, minus, jnp.zeros((LEFT - 2 * NB, 128), F32), plus], axis=0
            )
            plus = rhs + left + pltpu.roll(right, 128 - NB, 1)
            at = pl.ds(2 * i * step, NB, stride=stride)
            row = front[at, :]
            front[at, :] = jnp.where(near, row, 0.0) - jnp.dot(
                row, mat, precision=lax.Precision.HIGHEST, preferred_element_type=F32
            )
        levels.append((step, n))
        step, n = (2 * step, n // 2)

    last = eliminate([front[q * stride:q * stride + 1, :] for q in range(NB)])
    lanes = lane_iota(1)
    x0 = jnp.zeros((1, 128), F32)
    for q in range(NB):
        x0 = jnp.where(lanes == q, column(last[q], GL), x0)
    sol[8:9, :] = x0
    for step, n in reversed(levels):
        nxt = sol[pl.ds(8 + 2 * step, n, stride=2 * step), :]
        prv = sol[pl.ds(8, n, stride=2 * step), :]
        lanes = lane_iota(n)
        vec = pltpu.roll(nxt, NB, 1) + pltpu.roll(prv, LEFT, 1)
        vec = jnp.where(lanes == GL, -1.0, vec)
        x = jnp.zeros((n, 128), F32)
        for q in range(NB):
            row = front[pl.ds(q * stride + step, n, stride=2 * step), :]
            x = jnp.where(lanes == q, -jnp.sum(row * vec, axis=1, keepdims=True), x)
        sol[pl.ds(8 + step, n, stride=2 * step), :] = x
    out_ref[...] = -sol[8:8 + blocks, :]


def from_all(x, axis):
    size = lax.axis_size(axis)
    partner = lax.ppermute(x, axis, [(i, i ^ 1) for i in range(size)])
    pair = jnp.concatenate([x, partner], axis=0)
    parts = [pair]
    for k in range(2, size, 2):
        parts.append(lax.ppermute(pair, axis, [(i, i ^ k) for i in range(size)]))
    return parts


def sum_all(x, axis):
    size = lax.axis_size(axis)
    if size & (size - 1):
        return lax.psum(x, axis)
    parts = [x]
    for k in range(1, size):
        parts.append(lax.ppermute(x, axis, [(i, i ^ k) for i in range(size)]))
    while len(parts) > 1:
        parts = [parts[n] + parts[n + 1] for n in range(0, len(parts), 2)]
    return parts[0]


def basis_weights(u):
    square = u * u
    cube = square * u
    return jnp.stack(
        [
            (1.0 - u) ** 3 / 6.0,
            (3.0 * cube - 6.0 * square + 4.0) / 6.0,
            (-3.0 * cube + 3.0 * square + 3.0 * u + 1.0) / 6.0,
            cube / 6.0,
        ]
    )


def whole(shape):
    return pl.BlockSpec(shape, lambda r: (0,) * len(shape))


def local(
    ranges, valid_mask, match_tile, map_points, revolution_knot, spline_points, prior_weights
):
    revs, width, beams = ranges.shape
    knots = spline_points.shape[0]
    mapn = map_points.shape[0]
    blocks = knots // 4
    sectors = lax.axis_size("sector")
    sector = lax.axis_index("sector")
    total_revs = revs * lax.axis_size("rev")
    first = sector * width
    up = [(i, (i + 1) % sectors) for i in range(sectors)]
    down = [(j, i) for i, j in up]
    before = lax.ppermute(ranges[:, width - 1:, :], "sector", up)
    after = lax.ppermute(ranges[:, :1, :], "sector", down)

    rows = width + 2 * PAD
    column = (first - PAD + jnp.arange(rows, dtype=jnp.int32) + COLS) % COLS
    azimuth = 2.0 * jnp.pi * column.astype(F32) / COLS
    trig = jnp.stack([jnp.cos(azimuth), jnp.sin(azimuth)])
    trig = jnp.broadcast_to(trig[:, :, None], (2, rows, beams))
    beam = jnp.arange(beams, dtype=jnp.int32)

    def elevation(b):
        return -0.4 + 0.7 * b.astype(F32) / (beams - 1)

    up_e = elevation(jnp.minimum(beam + 1, beams - 1))
    dn_e = elevation(jnp.maximum(beam - 1, 0))
    mid_e = elevation(beam)
    beam_table = jnp.stack(
        [
            jnp.cos(mid_e), jnp.sin(mid_e), jnp.cos(up_e), jnp.cos(dn_e),
            jnp.sin(up_e), jnp.sin(dn_e), mid_e, mid_e,
        ]
    )
    weights = basis_weights(
        (first + jnp.arange(width, dtype=jnp.int32)).astype(F32) / COLS
    )
    basis = jnp.stack(
        [weights[j] * weights[i] for j, i in JPAIRS]
        + [weights[j] for j in range(4)]
        + [jnp.zeros_like(weights[0])] * 2
    )
    basis_hi = lax.reduce_precision(basis, 8, 7)
    basis = jnp.concatenate([basis_hi, basis - basis_hi], axis=0).astype(BF16)

    u = (first + width - 8 + jnp.arange(8, dtype=jnp.int32)).astype(F32) / COLS
    one = jnp.ones_like(u)
    slope = jnp.stack(
        [
            -0.5 * (1.0 - u) ** 2,
            (1.5 * u - 2.0) * u,
            (-1.5 * u + 1.0) * u + 0.5,
            0.5 * u * u,
        ]
    )
    bend = jnp.stack([1.0 - u, 3.0 * u - 2.0, 1.0 - 3.0 * u, u])
    third = jnp.stack([-one, 3.0 * one, -3.0 * one, one])
    pace = 8.0 / COLS
    a1, a2, a3 = (-pace * slope, pace**2 / 2.0 * bend, -(pace**3) / 6.0 * third)
    n0, n1, n2, n3 = (basis_weights(u), a1 + a2 + a3, 2.0 * a2 + 6.0 * a3, 6.0 * a3)
    mix = jnp.stack([n0 - n1 + n2 - n3, n1 - 2.0 * n2 + 3.0 * n3, n2 - 3.0 * n3, n3], axis=1)
    mix = jnp.broadcast_to(mix.reshape(16, 8, 1), (16, 8, beams))

    smem = pl.BlockSpec(memory_space=pltpu.SMEM)
    per_rev = pl.BlockSpec((1, width, beams), lambda r: (r, 0, 0))
    edge = pl.BlockSpec((1, 1, beams), lambda r: (r, 0, 0))
    normal_spec = pl.BlockSpec((3, 1, width, beams), lambda r: (0, r, 0, 0))
    two_revs = pl.BlockSpec((2, width, beams), lambda r: (r, 0, 0))
    point_spec = pl.BlockSpec((3, 1, rows, beams), lambda r: (0, r, 0, 0))
    two_points = pl.BlockSpec((3, 2, rows, beams), lambda r: (0, r, 0, 0))
    two_normals = pl.BlockSpec((3, 2, width, beams), lambda r: (0, r, 0, 0))
    params = pltpu.CompilerParams(
        dimension_semantics=("arbitrary",), vmem_limit_bytes=56 * 1024 * 1024
    )
    normals, resid, sums, points = pl.pallas_call(
        functools.partial(points_kernel, width=width, mapn=mapn, revs=revs),
        grid=(revs,),
        in_specs=[
            smem, smem, smem, smem, per_rev, per_rev, edge, edge,
            whole((3, mapn, beams)), whole((2, rows, beams)), whole((8, beams)),
        ],
        out_specs=[normal_spec, per_rev, whole((8, beams)), point_spec],
        out_shape=[
            jax.ShapeDtypeStruct((3, revs, width, beams), F32),
            jax.ShapeDtypeStruct((revs, width, beams), F32),
            jax.ShapeDtypeStruct((8, beams), F32),
            jax.ShapeDtypeStruct((3, revs, rows, beams), F32),
        ],
        scratch_shapes=[
            pltpu.VMEM((mapn * 4, beams), F32),
            pltpu.VMEM((256, beams), F32),
            pltpu.VMEM((256, beams), F32),
        ],
        compiler_params=params,
        name="points",
    )(
        first.reshape(1).astype(jnp.int32), revolution_knot, spline_points.T, (match_tile * 4).reshape(-1),
        ranges, valid_mask, before, after, jnp.transpose(map_points, (1, 0, 2)), trig, beam_table,
    )
    sums = sum_all(sums, "sector")
    knot_tag = jnp.where(sector == 0, revolution_knot, 0).astype(F32)
    share = pl.pallas_call(
        functools.partial(gram_kernel, width=width, scale=1.0 / (COLS * beams), revs=revs),
        grid=(revs // 2,),
        in_specs=[
            smem, two_points, two_revs, two_revs, two_normals, whole((8, beams)),
            whole((32, width)), whole((16, 8, beams)),
        ],
        out_specs=whole((4 * revs, beams)),
        out_shape=jax.ShapeDtypeStruct((4 * revs, beams), F32),
        scratch_shapes=[pltpu.VMEM((GRAD0 + 1, width, 128), BF16)] * 2
        + [pltpu.VMEM((8, 128), F32)],
        compiler_params=params,
        name="gram",
    )(knot_tag, points, valid_mask, resid, normals, sums, basis, mix)
    share = sum_all(share, "sector")
    shares = from_all(share, "rev")
    own = lax.axis_index("rev").reshape(1).astype(jnp.int32)
    prior = jnp.pad(prior_weights.reshape(blocks, NB), ((0, 0), (0, beams - NB)))
    update = pl.pallas_call(
        functools.partial(
            solve_kernel, blocks=blocks, revs=total_revs, sources=len(shares)
        ),
        in_specs=[smem] + [pl.BlockSpec(memory_space=pltpu.VMEM)] * (len(shares) + 2),
        out_shape=jax.ShapeDtypeStruct((blocks, 128), F32),
        scratch_shapes=[
            pltpu.VMEM((4 * total_revs, 128), F32),
            pltpu.VMEM((NB * (blocks + 8), 128), F32),
            pltpu.VMEM((2 * blocks + 16, 128), F32),
        ],
        compiler_params=pltpu.CompilerParams(vmem_limit_bytes=40 * 1024 * 1024),
        name="solve",
    )(own, *shares, prior, jnp.asarray(PLACE, BF16))
    return (normals, update[:, :NB].reshape(knots * 6))


def solution(mesh):
    return jax.shard_map(
        local,
        mesh=mesh,
        in_specs=(
            P("rev", "sector", None),
            P("rev", "sector", None),
            P("rev", "sector"),
            P(),
            P("rev"),
            P(),
            P(),
        ),
        out_specs=(P(None, "rev", "sector", None), P()),
        check_vma=False,
    )
```

```python
import functools

import jax
import jax.numpy as jnp
import numpy as np
from jax import lax
from jax.experimental import pallas as pl
from jax.experimental.pallas import tpu as pltpu
from jax.sharding import PartitionSpec as P

COLS = 2048
PAD = 8
F32 = jnp.float32
BF16 = jnp.bfloat16
NPROD = 26
GRAD0 = 20
PAIRS = [(a, e) for a in range(6) for e in range(a, 6) if (a, e) != (2, 5)]
PAIR_ID = {}
for _n, (_a, _e) in enumerate(PAIRS):
    PAIR_ID[_a, _e] = PAIR_ID[_e, _a] = _n
JPAIRS = [(j, i) for j in range(4) for i in range(j, 4)]
JPAIR_ID = {}
for _n, (_j, _i) in enumerate(JPAIRS):
    JPAIR_ID[_j, _i] = JPAIR_ID[_i, _j] = _n
NB = 24
GL = 64
LEFT = 104
KNOT_LANE = 27


def lane_iota(rows):
    return lax.broadcasted_iota(jnp.int32, (rows, 128), 1)


def points_kernel(
    first_ref, knot_ref, spline_ref, match_ref,
    range_ref, mask_ref, left_ref, right_ref, map_ref, trig_ref, beam_ref,
    normal_ref, resid_ref, sums_ref, pts,
    tiles, stage0, stage1,
    *, width, mapn, revs,
):
    r = pl.program_id(0)
    cosb = beam_ref[0:1, :]
    sinb = beam_ref[1:2, :]

    @pl.when(r == 0)
    def _():
        sums_ref[...] = jnp.zeros_like(sums_ref)

        def tile_body(t, carry):
            start = pl.multiple_of(t * 8, 8)
            for d in range(3):
                tiles[pl.ds(start * 4 + d, 8, stride=4), :] = map_ref[d, pl.ds(start, 8), :]
            return carry

        lax.fori_loop(0, mapn // 8, tile_body, 0, unroll=4)

    knot = knot_ref[r]
    cubic = []
    for d in range(3):
        c = [spline_ref[d, knot + j] for j in range(4)]
        cubic.append(
            (
                (c[0] + 4.0 * c[1] + c[2]) * (1.0 / 6.0),
                (c[2] - c[0]) * 0.5,
                (c[0] - 2.0 * c[1] + c[2]) * 0.5,
                (c[3] - c[0] + 3.0 * (c[1] - c[2])) * (1.0 / 6.0),
            )
        )
    first = first_ref[0]
    row_iota = lax.broadcasted_iota(jnp.int32, (8, 128), 0)

    def put_points(start, rng, column):
        u = (row_iota + column).astype(F32) * (1.0 / COLS)
        offset = [((k[3] * u + k[2]) * u + k[1]) * u + k[0] for k in cubic]
        rows = pl.ds(start, 8)
        flat = rng * cosb
        pts[0, 0, rows, :] = flat * trig_ref[0, rows, :] + offset[0]
        pts[1, 0, rows, :] = flat * trig_ref[1, rows, :] + offset[1]
        pts[2, 0, rows, :] = rng * sinb + offset[2]

    put_points(
        0, jnp.broadcast_to(left_ref[0], (8, 128)), jnp.where(first == 0, COLS, first) - PAD
    )
    put_points(
        width + PAD,
        jnp.broadcast_to(right_ref[0], (8, 128)),
        jnp.where(first + width == COLS, 0, first + width),
    )

    def put_chunk(t):
        for n in range(16):
            start = pl.multiple_of(t * 128 + 8 * n, 8)
            put_points(start + PAD, range_ref[0, pl.ds(start, 8), :], first + start)

    lanes = lane_iota(8)
    first_lane = lanes == 0
    last_lane = lanes == 127
    cup, cdn = (beam_ref[2:3, :], beam_ref[3:4, :])
    sup, sdn = (beam_ref[4:5, :], beam_ref[5:6, :])

    def gather(base, stage):
        here = r * width + base
        for c in range(64):
            row = pl.multiple_of(match_ref[here + c], 4)
            stage[pl.ds(4 * c, 4), :] = tiles[pl.ds(row, 4), :]

    def compute(base, stage, acc):
        sq, cnt = acc
        for s in range(8):
            start = base + 8 * s
            rng = range_ref[0, pl.ds(start, 8), :]
            up = jnp.where(last_lane, rng, pltpu.roll(rng, 127, 1))
            dn = jnp.where(first_lane, rng, pltpu.roll(rng, 1, 1))
            q = up * cup - dn * cdn
            bz = up * sup - dn * sdn
            bx = q * trig_ref[0, pl.ds(start + PAD, 8), :]
            by = q * trig_ref[1, pl.ds(start + PAD, 8), :]
            dx, dy, dz = (
                pts[d, 0, pl.ds(start + PAD + 1, 8), :] - pts[d, 0, pl.ds(start + PAD - 1, 8), :]
                for d in range(3)
            )
            cx = by * dz - bz * dy
            cy = bz * dx - bx * dz
            cz = bx * dy - by * dx
            inv = lax.rsqrt(cx * cx + cy * cy + cz * cz + 1.0)
            n = (cx * inv, cy * inv, cz * inv)
            res = jnp.zeros((8, 128), F32)
            for d in range(3):
                normal_ref[d, 0, pl.ds(start, 8), :] = n[d]
                target = stage[pl.ds(32 * s + d, 8, stride=4), :]
                res = res + n[d] * (pts[d, 0, pl.ds(start + PAD, 8), :] - target)
            resid_ref[0, pl.ds(start, 8), :] = res
            live = mask_ref[0, pl.ds(start, 8), :].astype(F32)
            sq = sq + live * res * res
            cnt = cnt + live
        return (sq, cnt)

    pairs = width // 128
    put_chunk(0)
    gather(0, stage0)

    def chunk_body(t, acc):
        put_chunk(jnp.minimum(t + 1, pairs - 1))
        base = pl.multiple_of(t * 128, 128)
        gather(base + 64, stage1)
        acc = compute(base, stage0, acc)
        gather(jnp.where(t + 1 < pairs, base + 128, 0), stage0)
        return compute(base + 64, stage1, acc)

    zero = jnp.zeros((8, 128), F32)
    sq, cnt = lax.fori_loop(0, pairs, chunk_body, (zero, zero))
    here = lane_iota(1) == r
    sums_ref[0:1, :] = jnp.where(here, jnp.sum(sq), sums_ref[0:1, :])
    sums_ref[1:2, :] = jnp.where(here, jnp.sum(cnt), sums_ref[1:2, :])


def basis_weights(u):
    square = u * u
    cube = square * u
    return [
        (1.0 - u) * (1.0 - u) * (1.0 - u) * (1.0 / 6.0),
        (3.0 * cube - 6.0 * square + 4.0) * (1.0 / 6.0),
        (-3.0 * cube + 3.0 * square + 3.0 * u + 1.0) * (1.0 / 6.0),
        cube * (1.0 / 6.0),
    ]


def level_weights(u):
    pace = 8.0 / COLS
    slope = (
        -0.5 * (1.0 - u) * (1.0 - u),
        (1.5 * u - 2.0) * u,
        (-1.5 * u + 1.0) * u + 0.5,
        0.5 * u * u,
    )
    bend = (1.0 - u, 3.0 * u - 2.0, 1.0 - 3.0 * u, u)
    third = (-1.0, 3.0, -3.0, 1.0)
    out = []
    for j, a0 in enumerate(basis_weights(u)):
        a1 = -pace * slope[j]
        a2 = pace**2 / 2.0 * bend[j]
        a3 = -(pace**3) / 6.0 * third[j]
        n1, n2, n3 = (a1 + a2 + a3, 2.0 * a2 + 6.0 * a3, 6.0 * a3)
        out += [a0 - n1 + n2 - n3, n1 - 2.0 * n2 + 3.0 * n3, n2 - 3.0 * n3, jnp.full_like(u, n3)]
    return out


def gram_kernel(
    first_ref, knot_ref,
    point_ref, mask_ref, resid_ref, normal_ref, sums_ref,
    out_ref,
    even, odd, grads, mix_ref, basis_ref,
    *, width, scale, revs,
):
    step = pl.program_id(0)

    @pl.when(step == 0)
    def _():
        row = lax.broadcasted_iota(jnp.int32, (8, 128), 0)
        mix = level_weights((row + (first_ref[0] + width - 8)).astype(F32) * (1.0 / COLS))
        for n in range(16):
            mix_ref[n] = mix[n]
        lane = lax.broadcasted_iota(jnp.int32, (8, width), 1)
        u = (lane + first_ref[0]).astype(F32) * (1.0 / COLS)
        weights = basis_weights(u)
        values = [weights[j] * weights[i] for j, i in JPAIRS] + [jnp.zeros_like(u)] * 6
        row = lax.broadcasted_iota(jnp.int32, (8, width), 0)
        table = []
        for half in range(2):
            total = jnp.zeros_like(u)
            for n in range(8):
                total = jnp.where(row == n, values[8 * half + n], total)
            table.append(total)
        table = jnp.concatenate(table, axis=0)
        high = table.astype(BF16)
        basis_ref[0:16, :] = high
        basis_ref[16:32, :] = (table - high.astype(F32)).astype(BF16)

    square, count = (sums_ref[0:1, :], sums_ref[1:2, :])
    inv_all = 1.0 / (square / jnp.maximum(count, 1.0) + 1e-06)
    lanes = lane_iota(16)
    row_lanes = lane_iota(1)

    def products(h, inv_spread, start, prods, sums):
        sums = list(sums)
        rows = pl.ds(start, 16)
        rows_pad = pl.ds(pl.multiple_of(start + PAD, 8), 16)
        px, py, pz = (point_ref[d, h, rows_pad, :] for d in range(3))
        nx, ny, nz = (normal_ref[d, h, rows, :] for d in range(3))
        res = resid_ref[h, rows, :]
        live = mask_ref[h, rows, :].astype(F32)
        robust = live / (1.0 + res * res * inv_spread)
        jac = (py * nz - pz * ny, pz * nx - px * nz, px * ny - py * nx, nx, ny, nz)
        wjac = [robust * j for j in jac]
        for n, (a, e) in enumerate(PAIRS):
            prods[n, rows, :] = (wjac[a] * jac[e]).astype(BF16)
        weighted = robust * res
        for part in range(2):
            span = slice(8 * part, 8 * part + 8)
            for a in range(6):
                total = jac[a][span] * weighted[span]
                for level in range(4):
                    total = sums[4 * a + level] + total
                    sums[4 * a + level] = total
        return sums

    def contract(k, prods, table):
        pair = jnp.concatenate([prods[2 * k], prods[2 * k + 1]], axis=1)
        part = jnp.dot(basis_ref[...], pair, preferred_element_type=F32)
        part = part[0:16, :] + part[16:32, :]
        for n in range(2):
            total = jnp.sum(part[:, 128 * n:128 * (n + 1)], axis=1, keepdims=True)
            table = jnp.where(lanes == 2 * k + n, total, table)
        return table

    def finish(rev, table, grads):
        table = table * scale
        grads = grads * scale
        tag = jnp.where(first_ref[0] == 0, knot_ref[rev], 0).astype(F32)
        out = []
        for j in range(4):
            line = jnp.where(row_lanes == KNOT_LANE, tag, grads[j:j + 1, :])
            for i in range(4):
                piece = table[JPAIR_ID[j, i]:JPAIR_ID[j, i] + 1, :]
                piece = jnp.where(row_lanes < GRAD0, piece, 0.0)
                if i:
                    piece = pltpu.roll(piece, 32 * i, 1)
                line = line + piece
            out.append(line)
        out_ref[pl.ds(pl.multiple_of(rev * 4, 4), 4), :] = jnp.concatenate(out, axis=0)

    trips = 2
    items = width // 32 // trips
    empty = jnp.zeros((16, 128), F32)
    pairs = (GRAD0 + 1) // 2
    each = -(-pairs // trips)

    def gradient(sums):
        out = jnp.zeros((8, 128), F32)
        for j in range(4):
            total = jnp.zeros((8, 128), F32)
            for a in range(6):
                value = mix_ref[4 * j] * sums[4 * a]
                for level in range(1, 4):
                    value = value + mix_ref[4 * j + level] * sums[4 * a + level]
                value = jnp.sum(value, axis=1, keepdims=True)
                total = jnp.where(lanes8 == GRAD0 + a, value, total)
            out = jnp.where(lane_rows == j, jnp.sum(total, axis=0, keepdims=True), out)
        return out

    lanes8 = lane_iota(8)
    lane_rows = lax.broadcasted_iota(jnp.int32, (8, 128), 0)
    for h in range(2):
        now, done = (even, odd) if h == 0 else (odd, even)
        r = 2 * step + h
        inv_spread = jnp.sum(jnp.where(row_lanes == r, inv_all, 0.0), axis=1, keepdims=True)
        inv_spread = jnp.broadcast_to(inv_spread, (16, 128))

        def body(t, carry, h=h, now=now, done=done, inv_spread=inv_spread):
            table, sums = (carry[0], carry[1:])
            for u in range(max(each, items)):
                if u < each:
                    table = contract(jnp.minimum(t * each + u, pairs - 1), done, table)
                if u < items:
                    for part in range(2):
                        start = pl.multiple_of((t * items + u) * 32 + 16 * part, 16)
                        sums = products(h, inv_spread, start, now, sums)
            return (table, *sums)

        zero = jnp.zeros((8, 128), F32)
        table, *sums = lax.fori_loop(0, trips, body, (empty,) + (zero,) * 24)
        finish(jnp.maximum(r - 1, 0), table, grads[...])
        grads[...] = gradient(sums)

    @pl.when(step == revs // 2 - 1)
    def _():
        table = lax.fori_loop(0, pairs, lambda k, t: contract(k, odd, t), empty, unroll=True)
        finish(revs - 1, table, grads[...])


def placement():
    mats = []
    index = {}
    for a in range(6):
        for s in range(4):
            for wrap in range(2 if s else 1):
                m = np.zeros((128, 128), np.float32)
                for i in range(4):
                    for e in range(6):
                        lane = 6 * (i + s) + e - NB * wrap
                        if (a, e) in PAIR_ID:
                            m[32 * i + PAIR_ID[a, e], lane % 128] = 1.0
                        else:
                            m[32 * i + PAIR_ID[0, 3], lane % 128] = -1.0
                            m[32 * i + PAIR_ID[1, 4], lane % 128] = -1.0
                m[GRAD0 + a, GL] = 1.0
                index[a, s, wrap] = len(mats)
                mats.append(m)
    return np.stack(mats), index


PLACE, PLACE_ID = placement()


def split3(x):
    a = x.astype(BF16)
    b = x - a.astype(F32)
    m = b.astype(BF16)
    return (a, m, (b - m.astype(F32)).astype(BF16))


def solve_kernel(own_ref, *refs, blocks, revs, sources):
    shares = refs[:sources]
    prior_ref, place_ref, out_ref, x_ref, front, sol = refs[sources:]
    each = 2 * revs // sources
    for k in range(sources):
        for side in range(2):
            src = own_ref[0] ^ (2 * k + side)
            x_ref[pl.ds(pl.multiple_of(src * each, 8), each), :] = shares[k][
                side * each:(side + 1) * each, :
            ]
    stride = blocks + 8
    knots = 4 * blocks
    lanes_b = lane_iota(blocks)

    knot_col = x_ref[pl.ds(0, revs, stride=4), :][:, KNOT_LANE:KNOT_LANE + 1]
    knot_col = jnp.broadcast_to((knot_col + 0.5).astype(jnp.int32), (revs, knots))
    slot = lax.broadcasted_iota(jnp.int32, (revs, knots), 1)
    s_of = slot // blocks
    m_of = slot - s_of * blocks
    dims = (((0,), (0,)), ((), ()))
    sums = {}
    for shift in range(2):
        hot = jnp.where(knot_col == 4 * (m_of - shift) + s_of, 1.0, 0.0).astype(BF16)
        for j in range(4):
            parts = split3(x_ref[pl.ds(j, revs, stride=4), :])
            total = None
            for part in parts:
                y = lax.dot_general(hot, part, dims, preferred_element_type=F32)
                total = y if total is None else total + y
            sums[shift, j] = split3(total)

    rows = {}
    for a in range(6):
        for s in range(4):
            for wrap in range(2 if s else 1):
                js = range(4 - s, 4) if wrap else range(4 - s)
                lhs = jnp.concatenate(
                    [sums[wrap, j][k][s * blocks:(s + 1) * blocks] for k in range(3) for j in js],
                    axis=0,
                )
                y = jnp.dot(lhs, place_ref[PLACE_ID[a, s, wrap]], preferred_element_type=F32)
                count = len(js) * blocks
                y = y[0:count] + y[count:2 * count] + y[2 * count:3 * count]
                for n, j in enumerate(js):
                    q = 6 * ((s + j) % 4) + a
                    part = y[n * blocks:(n + 1) * blocks]
                    rows[q] = part if q not in rows else rows[q] + part
    prior = prior_ref[...]
    for q in range(NB):
        front[q * stride:q * stride + blocks, :] = rows[q] + jnp.where(lanes_b == q, prior, 0.0)

    def column(x, k):
        return jnp.broadcast_to(x[:, k:k + 1], x.shape)

    def eliminate(mat):
        for k in range(NB):
            pivot = mat[k] / column(mat[k], k)
            mat = [pivot if q == k else mat[q] - column(mat[q], k) * pivot for q in range(NB)]
        return mat

    sol[...] = jnp.zeros_like(sol)
    levels = []
    step = 1
    n = blocks // 2
    lanes = lane_iota(NB)
    near = (lanes < NB) | (lanes == GL)
    zeros = jnp.zeros((NB, 128), F32)
    while n >= 1:
        odd = eliminate([front[pl.ds(q * stride + step, n, stride=2 * step), :] for q in range(NB)])
        for q in range(NB):
            front[pl.ds(q * stride + step, n, stride=2 * step), :] = odd[q]
        plus = zeros
        for i in range(n):
            x = front[pl.ds((2 * i + 1) * step, NB, stride=stride), :]
            right = jnp.where((lanes >= NB) & (lanes < 2 * NB), x, 0.0)
            left = jnp.where(lanes >= LEFT, x, 0.0)
            rhs = jnp.where(lanes == GL, x, 0.0)
            minus = rhs + right + pltpu.roll(left, NB, 1)
            mat = jnp.concatenate(
                [zeros, minus, jnp.zeros((LEFT - 2 * NB, 128), F32), plus], axis=0
            )
            plus = rhs + left + pltpu.roll(right, 128 - NB, 1)
            at = pl.ds(2 * i * step, NB, stride=stride)
            row = front[at, :]
            front[at, :] = jnp.where(near, row, 0.0) - jnp.dot(
                row, mat, precision=lax.Precision.HIGHEST, preferred_element_type=F32
            )
        levels.append((step, n))
        step, n = (2 * step, n // 2)

    last = eliminate([front[q * stride:q * stride + 1, :] for q in range(NB)])
    lanes = lane_iota(1)
    x0 = jnp.zeros((1, 128), F32)
    for q in range(NB):
        x0 = jnp.where(lanes == q, column(last[q], GL), x0)
    sol[8:9, :] = x0
    for step, n in reversed(levels):
        nxt = sol[pl.ds(8 + 2 * step, n, stride=2 * step), :]
        prv = sol[pl.ds(8, n, stride=2 * step), :]
        lanes = lane_iota(n)
        vec = pltpu.roll(nxt, NB, 1) + pltpu.roll(prv, LEFT, 1)
        vec = jnp.where(lanes == GL, -1.0, vec)
        x = jnp.zeros((n, 128), F32)
        for q in range(NB):
            row = front[pl.ds(q * stride + step, n, stride=2 * step), :]
            x = jnp.where(lanes == q, -jnp.sum(row * vec, axis=1, keepdims=True), x)
        sol[pl.ds(8 + step, n, stride=2 * step), :] = x
    out_ref[...] = -sol[8:8 + blocks, :]


def from_all(x, axis):
    size = lax.axis_size(axis)
    partner = lax.ppermute(x, axis, [(i, i ^ 1) for i in range(size)])
    pair = jnp.concatenate([x, partner], axis=0)
    parts = [pair]
    for k in range(2, size, 2):
        parts.append(lax.ppermute(pair, axis, [(i, i ^ k) for i in range(size)]))
    return parts


def sum_all(x, axis):
    size = lax.axis_size(axis)
    if size & (size - 1):
        return lax.psum(x, axis)
    parts = [x]
    for k in range(1, size):
        parts.append(lax.ppermute(x, axis, [(i, i ^ k) for i in range(size)]))
    while len(parts) > 1:
        parts = [parts[n] + parts[n + 1] for n in range(0, len(parts), 2)]
    return parts[0]


def beam_rows(beams):
    beam = np.arange(beams)
    rows = []
    for near in (beam, np.minimum(beam + 1, beams - 1), np.maximum(beam - 1, 0)):
        angle = np.float32(-0.4) + np.float32(0.7) * near.astype(np.float32) / np.float32(beams - 1)
        rows.append((np.cos(angle.astype(np.float64)), np.sin(angle.astype(np.float64))))
    (cos, sin), (cos_up, sin_up), (cos_dn, sin_dn) = rows
    return np.stack([cos, sin, cos_up, cos_dn, sin_up, sin_dn, cos, sin]).astype(np.float32)


def whole(shape):
    return pl.BlockSpec(shape, lambda r: (0,) * len(shape))


def local(
    ranges, valid_mask, match_tile, map_points, revolution_knot, spline_points, prior_weights
):
    revs, width, beams = ranges.shape
    knots = spline_points.shape[0]
    mapn = map_points.shape[0]
    blocks = knots // 4
    sectors = lax.axis_size("sector")
    sector = lax.axis_index("sector")
    total_revs = revs * lax.axis_size("rev")
    first = sector * width
    first_column = first.reshape(1).astype(jnp.int32)
    up = [(i, (i + 1) % sectors) for i in range(sectors)]
    down = [(j, i) for i, j in up]
    before = lax.ppermute(ranges[:, width - 1:, :], "sector", up)
    after = lax.ppermute(ranges[:, :1, :], "sector", down)

    rows = width + 2 * PAD
    column = (first - PAD + jnp.arange(rows, dtype=jnp.int32) + COLS) % COLS
    azimuth = 2.0 * jnp.pi * column.astype(F32) / COLS
    trig = jnp.stack([jnp.cos(azimuth), jnp.sin(azimuth)])
    trig = jnp.broadcast_to(trig[:, :, None], (2, rows, beams))
    beam_table = jnp.asarray(beam_rows(beams))

    smem = pl.BlockSpec(memory_space=pltpu.SMEM)
    per_rev = pl.BlockSpec((1, width, beams), lambda r: (r, 0, 0))
    edge = pl.BlockSpec((1, 1, beams), lambda r: (r, 0, 0))
    normal_spec = pl.BlockSpec((3, 1, width, beams), lambda r: (0, r, 0, 0))
    two_revs = pl.BlockSpec((2, width, beams), lambda r: (r, 0, 0))
    point_spec = pl.BlockSpec((3, 1, rows, beams), lambda r: (0, r, 0, 0))
    two_points = pl.BlockSpec((3, 2, rows, beams), lambda r: (0, r, 0, 0))
    two_normals = pl.BlockSpec((3, 2, width, beams), lambda r: (0, r, 0, 0))
    params = pltpu.CompilerParams(
        dimension_semantics=("arbitrary",), vmem_limit_bytes=56 * 1024 * 1024
    )
    normals, resid, sums, points = pl.pallas_call(
        functools.partial(points_kernel, width=width, mapn=mapn, revs=revs),
        grid=(revs,),
        in_specs=[
            smem, smem, smem, smem, per_rev, per_rev, edge, edge,
            whole((3, mapn, beams)), whole((2, rows, beams)), whole((8, beams)),
        ],
        out_specs=[normal_spec, per_rev, whole((8, beams)), point_spec],
        out_shape=[
            jax.ShapeDtypeStruct((3, revs, width, beams), F32),
            jax.ShapeDtypeStruct((revs, width, beams), F32),
            jax.ShapeDtypeStruct((8, beams), F32),
            jax.ShapeDtypeStruct((3, revs, rows, beams), F32),
        ],
        scratch_shapes=[
            pltpu.VMEM((mapn * 4, beams), F32),
            pltpu.VMEM((256, beams), F32),
            pltpu.VMEM((256, beams), F32),
        ],
        compiler_params=params,
        name="points",
    )(
        first_column, revolution_knot, spline_points.T, (match_tile * 4).reshape(-1),
        ranges, valid_mask, before, after, jnp.transpose(map_points, (1, 0, 2)), trig, beam_table,
    )
    sums = sum_all(sums, "sector")
    share = pl.pallas_call(
        functools.partial(gram_kernel, width=width, scale=1.0 / (COLS * beams), revs=revs),
        grid=(revs // 2,),
        in_specs=[
            smem, smem, two_points, two_revs, two_revs, two_normals, whole((8, beams)),
        ],
        out_specs=whole((4 * revs, beams)),
        out_shape=jax.ShapeDtypeStruct((4 * revs, beams), F32),
        scratch_shapes=[pltpu.VMEM((GRAD0, width, 128), BF16)] * 2
        + [
            pltpu.VMEM((8, 128), F32),
            pltpu.VMEM((16, 8, 128), F32),
            pltpu.VMEM((32, width), BF16),
        ],
        compiler_params=params,
        name="gram",
    )(first_column, revolution_knot, points, valid_mask, resid, normals, sums)
    share = sum_all(share, "sector")
    shares = from_all(share, "rev")
    own = lax.axis_index("rev").reshape(1).astype(jnp.int32)
    prior = jnp.pad(prior_weights.reshape(blocks, NB), ((0, 0), (0, beams - NB)))
    update = pl.pallas_call(
        functools.partial(
            solve_kernel, blocks=blocks, revs=total_revs, sources=len(shares)
        ),
        in_specs=[smem] + [pl.BlockSpec(memory_space=pltpu.VMEM)] * (len(shares) + 2),
        out_shape=jax.ShapeDtypeStruct((blocks, 128), F32),
        scratch_shapes=[
            pltpu.VMEM((4 * total_revs, 128), F32),
            pltpu.VMEM((NB * (blocks + 8), 128), F32),
            pltpu.VMEM((2 * blocks + 16, 128), F32),
        ],
        compiler_params=pltpu.CompilerParams(vmem_limit_bytes=40 * 1024 * 1024),
        name="solve",
    )(own, *shares, prior, jnp.asarray(PLACE, BF16))
    return (normals, update[:, :NB].reshape(knots * 6))


def solution(mesh):
    return jax.shard_map(
        local,
        mesh=mesh,
        in_specs=(
            P("rev", "sector", None),
            P("rev", "sector", None),
            P("rev", "sector"),
            P(),
            P("rev"),
            P(),
            P(),
        ),
        out_specs=(P(None, "rev", "sector", None), P()),
        check_vma=False,
    )
```

```python
import functools

import jax
import jax.numpy as jnp
import numpy as np
from jax import lax
from jax.experimental import pallas as pl
from jax.experimental.pallas import tpu as pltpu
from jax.sharding import PartitionSpec as P

COLS = 2048
PAD = 8
F32 = jnp.float32
BF16 = jnp.bfloat16
NPROD = 26
GRAD0 = 20
PAIRS = [(a, e) for a in range(6) for e in range(a, 6) if (a, e) != (2, 5)]
PAIR_ID = {}
for _n, (_a, _e) in enumerate(PAIRS):
    PAIR_ID[_a, _e] = PAIR_ID[_e, _a] = _n
JPAIRS = [(j, i) for j in range(4) for i in range(j, 4)]
JPAIR_ID = {}
for _n, (_j, _i) in enumerate(JPAIRS):
    JPAIR_ID[_j, _i] = JPAIR_ID[_i, _j] = _n
NB = 24
GL = 64
LEFT = 104
KNOT_LANE = 27


def lane_iota(rows):
    return lax.broadcasted_iota(jnp.int32, (rows, 128), 1)


def points_kernel(
    first_ref, knot_ref, spline_ref, match_ref,
    range_ref, mask_ref, left_ref, right_ref, map_ref, trig_ref, beam_ref,
    normal_ref, resid_ref, sums_ref, pts,
    tiles, stage0, stage1,
    *, width, mapn, revs,
):
    r = pl.program_id(0)
    cosb = beam_ref[0:1, :]
    sinb = beam_ref[1:2, :]

    @pl.when(r == 0)
    def _():
        sums_ref[...] = jnp.zeros_like(sums_ref)

        def tile_body(t, carry):
            start = pl.multiple_of(t * 8, 8)
            for d in range(3):
                tiles[pl.ds(start * 4 + d, 8, stride=4), :] = map_ref[d, pl.ds(start, 8), :]
            return carry

        lax.fori_loop(0, mapn // 8, tile_body, 0, unroll=4)

    knot = knot_ref[r]
    cubic = []
    for d in range(3):
        c = [spline_ref[d, knot + j] for j in range(4)]
        cubic.append(
            (
                (c[0] + 4.0 * c[1] + c[2]) * (1.0 / 6.0),
                (c[2] - c[0]) * 0.5,
                (c[0] - 2.0 * c[1] + c[2]) * 0.5,
                (c[3] - c[0] + 3.0 * (c[1] - c[2])) * (1.0 / 6.0),
            )
        )
    first = first_ref[0]
    row_iota = lax.broadcasted_iota(jnp.int32, (8, 128), 0)

    def put_points(start, rng, column):
        u = (row_iota + column).astype(F32) * (1.0 / COLS)
        offset = [((k[3] * u + k[2]) * u + k[1]) * u + k[0] for k in cubic]
        rows = pl.ds(start, 8)
        flat = rng * cosb
        pts[0, 0, rows, :] = flat * trig_ref[0, rows, :] + offset[0]
        pts[1, 0, rows, :] = flat * trig_ref[1, rows, :] + offset[1]
        pts[2, 0, rows, :] = rng * sinb + offset[2]

    put_points(
        0, jnp.broadcast_to(left_ref[0], (8, 128)), jnp.where(first == 0, COLS, first) - PAD
    )
    put_points(
        width + PAD,
        jnp.broadcast_to(right_ref[0], (8, 128)),
        jnp.where(first + width == COLS, 0, first + width),
    )

    def put_chunk(t):
        for n in range(16):
            start = pl.multiple_of(t * 128 + 8 * n, 8)
            put_points(start + PAD, range_ref[0, pl.ds(start, 8), :], first + start)

    lanes = lane_iota(8)
    first_lane = lanes == 0
    last_lane = lanes == 127
    cup, cdn = (beam_ref[2:3, :], beam_ref[3:4, :])
    sup, sdn = (beam_ref[4:5, :], beam_ref[5:6, :])

    def gather(base, stage):
        here = r * width + base
        for c in range(64):
            row = pl.multiple_of(match_ref[here + c], 4)
            stage[pl.ds(4 * c, 4), :] = tiles[pl.ds(row, 4), :]

    def compute(base, stage, acc):
        sq, cnt = acc
        for s in range(8):
            start = base + 8 * s
            rng = range_ref[0, pl.ds(start, 8), :]
            up = jnp.where(last_lane, rng, pltpu.roll(rng, 127, 1))
            dn = jnp.where(first_lane, rng, pltpu.roll(rng, 1, 1))
            q = up * cup - dn * cdn
            bz = up * sup - dn * sdn
            bx = q * trig_ref[0, pl.ds(start + PAD, 8), :]
            by = q * trig_ref[1, pl.ds(start + PAD, 8), :]
            dx, dy, dz = (
                pts[d, 0, pl.ds(start + PAD + 1, 8), :] - pts[d, 0, pl.ds(start + PAD - 1, 8), :]
                for d in range(3)
            )
            cx = by * dz - bz * dy
            cy = bz * dx - bx * dz
            cz = bx * dy - by * dx
            inv = lax.rsqrt(cx * cx + cy * cy + cz * cz + 1.0)
            n = (cx * inv, cy * inv, cz * inv)
            res = jnp.zeros((8, 128), F32)
            for d in range(3):
                normal_ref[d, 0, pl.ds(start, 8), :] = n[d]
                target = stage[pl.ds(32 * s + d, 8, stride=4), :]
                res = res + n[d] * (pts[d, 0, pl.ds(start + PAD, 8), :] - target)
            resid_ref[0, pl.ds(start, 8), :] = res
            live = mask_ref[0, pl.ds(start, 8), :].astype(F32)
            sq = sq + live * res * res
            cnt = cnt + live
        return (sq, cnt)

    pairs = width // 128
    put_chunk(0)
    gather(0, stage0)

    def chunk_body(t, acc):
        put_chunk(jnp.minimum(t + 1, pairs - 1))
        base = pl.multiple_of(t * 128, 128)
        gather(base + 64, stage1)
        acc = compute(base, stage0, acc)
        gather(jnp.where(t + 1 < pairs, base + 128, 0), stage0)
        return compute(base + 64, stage1, acc)

    zero = jnp.zeros((8, 128), F32)
    sq, cnt = lax.fori_loop(0, pairs, chunk_body, (zero, zero))
    here = lane_iota(1) == r
    sums_ref[0:1, :] = jnp.where(here, jnp.sum(sq), sums_ref[0:1, :])
    sums_ref[1:2, :] = jnp.where(here, jnp.sum(cnt), sums_ref[1:2, :])


def basis_weights(u):
    square = u * u
    cube = square * u
    return [
        (1.0 - u) * (1.0 - u) * (1.0 - u) * (1.0 / 6.0),
        (3.0 * cube - 6.0 * square + 4.0) * (1.0 / 6.0),
        (-3.0 * cube + 3.0 * square + 3.0 * u + 1.0) * (1.0 / 6.0),
        cube * (1.0 / 6.0),
    ]


def level_weights(u):
    pace = 8.0 / COLS
    slope = (
        -0.5 * (1.0 - u) * (1.0 - u),
        (1.5 * u - 2.0) * u,
        (-1.5 * u + 1.0) * u + 0.5,
        0.5 * u * u,
    )
    bend = (1.0 - u, 3.0 * u - 2.0, 1.0 - 3.0 * u, u)
    third = (-1.0, 3.0, -3.0, 1.0)
    out = []
    for j, a0 in enumerate(basis_weights(u)):
        a1 = -pace * slope[j]
        a2 = pace**2 / 2.0 * bend[j]
        a3 = -(pace**3) / 6.0 * third[j]
        n1, n2, n3 = (a1 + a2 + a3, 2.0 * a2 + 6.0 * a3, 6.0 * a3)
        out += [a0 - n1 + n2 - n3, n1 - 2.0 * n2 + 3.0 * n3, n2 - 3.0 * n3, jnp.full_like(u, n3)]
    return out


def gram_kernel(
    first_ref, knot_ref,
    point_ref, mask_ref, resid_ref, normal_ref, sums_ref,
    out_ref,
    even, odd, grads, mix_ref, basis_ref,
    *, width, scale, revs,
):
    step = pl.program_id(0)

    @pl.when(step == 0)
    def _():
        row = lax.broadcasted_iota(jnp.int32, (8, 128), 0)
        mix = level_weights((row + (first_ref[0] + width - 8)).astype(F32) * (1.0 / COLS))
        for n in range(16):
            mix_ref[n] = mix[n]
        lane = lax.broadcasted_iota(jnp.int32, (8, width), 1)
        u = (lane + first_ref[0]).astype(F32) * (1.0 / COLS)
        weights = basis_weights(u)
        values = [weights[j] * weights[i] for j, i in JPAIRS] + [jnp.zeros_like(u)] * 6
        row = lax.broadcasted_iota(jnp.int32, (8, width), 0)
        table = []
        for half in range(2):
            total = jnp.zeros_like(u)
            for n in range(8):
                total = jnp.where(row == n, values[8 * half + n], total)
            table.append(total)
        table = jnp.concatenate(table, axis=0)
        high = table.astype(BF16)
        basis_ref[0:16, :] = high
        basis_ref[16:32, :] = (table - high.astype(F32)).astype(BF16)

    square, count = (sums_ref[0:1, :], sums_ref[1:2, :])
    inv_all = 1.0 / (square / jnp.maximum(count, 1.0) + 1e-06)
    lanes = lane_iota(16)
    row_lanes = lane_iota(1)

    def products(h, inv_spread, start, prods, sums):
        sums = list(sums)
        rows = pl.ds(start, 16)
        rows_pad = pl.ds(pl.multiple_of(start + PAD, 8), 16)
        px, py, pz = (point_ref[d, h, rows_pad, :] for d in range(3))
        nx, ny, nz = (normal_ref[d, h, rows, :] for d in range(3))
        res = resid_ref[h, rows, :]
        live = mask_ref[h, rows, :].astype(F32)
        robust = live / (1.0 + res * res * inv_spread)
        jac = (py * nz - pz * ny, pz * nx - px * nz, px * ny - py * nx, nx, ny, nz)
        wjac = [robust * j for j in jac]
        for n, (a, e) in enumerate(PAIRS):
            prods[n, rows, :] = (wjac[a] * jac[e]).astype(BF16)
        weighted = robust * res
        for part in range(2):
            span = slice(8 * part, 8 * part + 8)
            for a in range(6):
                total = jac[a][span] * weighted[span]
                for level in range(4):
                    total = sums[4 * a + level] + total
                    sums[4 * a + level] = total
        return sums

    def contract(k, prods, table):
        pair = jnp.concatenate([prods[2 * k], prods[2 * k + 1]], axis=1)
        part = jnp.dot(basis_ref[...], pair, preferred_element_type=F32)
        part = part[0:16, :] + part[16:32, :]
        for n in range(2):
            total = jnp.sum(part[:, 128 * n:128 * (n + 1)], axis=1, keepdims=True)
            table = jnp.where(lanes == 2 * k + n, total, table)
        return table

    def finish(rev, table, grads):
        table = table * scale
        grads = grads * scale
        tag = jnp.where(first_ref[0] == 0, knot_ref[rev], 0).astype(F32)
        out = []
        for j in range(4):
            line = jnp.where(row_lanes == KNOT_LANE, tag, grads[j:j + 1, :])
            for i in range(4):
                piece = table[JPAIR_ID[j, i]:JPAIR_ID[j, i] + 1, :]
                piece = jnp.where(row_lanes < GRAD0, piece, 0.0)
                if i:
                    piece = pltpu.roll(piece, 32 * i, 1)
                line = line + piece
            out.append(line)
        at = pl.ds(pl.multiple_of(rev // 2 * 8, 8), 8)
        side = lax.broadcasted_iota(jnp.int32, (8, 128), 0) // 4
        out_ref[at, :] = jnp.where(
            side == rev - rev // 2 * 2, jnp.concatenate(out + out, axis=0), out_ref[at, :]
        )

    trips = 2
    items = width // 32 // trips
    empty = jnp.zeros((16, 128), F32)
    pairs = (GRAD0 + 1) // 2
    each = -(-pairs // trips)

    def gradient(sums):
        out = jnp.zeros((8, 128), F32)
        for j in range(4):
            total = jnp.zeros((8, 128), F32)
            for a in range(6):
                value = mix_ref[4 * j] * sums[4 * a]
                for level in range(1, 4):
                    value = value + mix_ref[4 * j + level] * sums[4 * a + level]
                value = jnp.sum(value, axis=1, keepdims=True)
                total = jnp.where(lanes8 == GRAD0 + a, value, total)
            out = jnp.where(lane_rows == j, jnp.sum(total, axis=0, keepdims=True), out)
        return out

    lanes8 = lane_iota(8)
    lane_rows = lax.broadcasted_iota(jnp.int32, (8, 128), 0)
    for h in range(2):
        now, done = (even, odd) if h == 0 else (odd, even)
        r = 2 * step + h
        inv_spread = jnp.sum(jnp.where(row_lanes == r, inv_all, 0.0), axis=1, keepdims=True)
        inv_spread = jnp.broadcast_to(inv_spread, (16, 128))

        def body(t, carry, h=h, now=now, done=done, inv_spread=inv_spread):
            table, sums = (carry[0], carry[1:])
            for u in range(max(each, items)):
                if u < each:
                    table = contract(jnp.minimum(t * each + u, pairs - 1), done, table)
                if u < items:
                    for part in range(2):
                        start = pl.multiple_of((t * items + u) * 32 + 16 * part, 16)
                        sums = products(h, inv_spread, start, now, sums)
            return (table, *sums)

        zero = jnp.zeros((8, 128), F32)
        table, *sums = lax.fori_loop(0, trips, body, (empty,) + (zero,) * 24)
        finish(jnp.maximum(r - 1, 0), table, grads[...])
        grads[...] = gradient(sums)

    @pl.when(step == revs // 2 - 1)
    def _():
        table = lax.fori_loop(0, pairs, lambda k, t: contract(k, odd, t), empty, unroll=True)
        finish(revs - 1, table, grads[...])


def placement():
    mats = []
    index = {}
    for a in range(6):
        for s in range(4):
            for wrap in range(2 if s else 1):
                m = np.zeros((128, 128), np.float32)
                for i in range(4):
                    for e in range(6):
                        lane = 6 * (i + s) + e - NB * wrap
                        if (a, e) in PAIR_ID:
                            m[32 * i + PAIR_ID[a, e], lane % 128] = 1.0
                        else:
                            m[32 * i + PAIR_ID[0, 3], lane % 128] = -1.0
                            m[32 * i + PAIR_ID[1, 4], lane % 128] = -1.0
                m[GRAD0 + a, GL] = 1.0
                index[a, s, wrap] = len(mats)
                mats.append(m)
    return np.stack(mats), index


PLACE, PLACE_ID = placement()


def split3(x):
    a = x.astype(BF16)
    b = x - a.astype(F32)
    m = b.astype(BF16)
    return (a, m, (b - m.astype(F32)).astype(BF16))


def solve_kernel(own_ref, *refs, blocks, revs, sources):
    shares = refs[:sources]
    prior_ref, place_ref, out_ref, x_ref, front, sol = refs[sources:]
    each = 2 * revs // sources
    for k in range(sources):
        for side in range(2):
            src = own_ref[0] ^ (2 * k + side)
            x_ref[pl.ds(pl.multiple_of(src * each, 8), each), :] = shares[k][
                side * each:(side + 1) * each, :
            ]
    stride = blocks + 8
    knots = 4 * blocks
    lanes_b = lane_iota(blocks)

    knot_col = x_ref[pl.ds(0, revs, stride=4), :][:, KNOT_LANE:KNOT_LANE + 1]
    knot_col = jnp.broadcast_to((knot_col + 0.5).astype(jnp.int32), (revs, knots))
    slot = lax.broadcasted_iota(jnp.int32, (revs, knots), 1)
    s_of = slot // blocks
    m_of = slot - s_of * blocks
    dims = (((0,), (0,)), ((), ()))
    sums = {}
    for shift in range(2):
        hot = jnp.where(knot_col == 4 * (m_of - shift) + s_of, 1.0, 0.0).astype(BF16)
        for j in range(4):
            parts = split3(x_ref[pl.ds(j, revs, stride=4), :])
            total = None
            for part in parts:
                y = lax.dot_general(hot, part, dims, preferred_element_type=F32)
                total = y if total is None else total + y
            sums[shift, j] = split3(total)

    rows = {}
    for a in range(6):
        for s in range(4):
            for wrap in range(2 if s else 1):
                js = range(4 - s, 4) if wrap else range(4 - s)
                lhs = jnp.concatenate(
                    [sums[wrap, j][k][s * blocks:(s + 1) * blocks] for k in range(3) for j in js],
                    axis=0,
                )
                y = jnp.dot(lhs, place_ref[PLACE_ID[a, s, wrap]], preferred_element_type=F32)
                count = len(js) * blocks
                y = y[0:count] + y[count:2 * count] + y[2 * count:3 * count]
                for n, j in enumerate(js):
                    q = 6 * ((s + j) % 4) + a
                    part = y[n * blocks:(n + 1) * blocks]
                    rows[q] = part if q not in rows else rows[q] + part
    prior = prior_ref[...]
    for q in range(NB):
        front[q * stride:q * stride + blocks, :] = rows[q] + jnp.where(lanes_b == q, prior, 0.0)

    def column(x, k):
        return jnp.broadcast_to(x[:, k:k + 1], x.shape)

    def eliminate(mat):
        for k in range(NB):
            pivot = mat[k] / column(mat[k], k)
            mat = [pivot if q == k else mat[q] - column(mat[q], k) * pivot for q in range(NB)]
        return mat

    def split3f(x):
        high = x.astype(BF16).astype(F32)
        mid = (x - high).astype(BF16).astype(F32)
        return (high, mid, x - high - mid)

    def meet(row, minus, plus):
        total = None
        for depth in (2, 1, 0):
            mat = jnp.concatenate(
                [zeros, minus[depth], jnp.zeros((LEFT - 2 * NB, 128), F32), plus[depth]], axis=0
            )
            lhs = jnp.concatenate(row[:3 - depth], axis=0).astype(BF16)
            part = jnp.dot(lhs, mat.astype(BF16), preferred_element_type=F32)
            for n in range(2 - depth, -1, -1):
                piece = part[n * NB:(n + 1) * NB]
                total = piece if total is None else total + piece
        return total

    sol[...] = jnp.zeros_like(sol)
    levels = []
    step = 1
    n = blocks // 2
    lanes = lane_iota(NB)
    near = (lanes < NB) | (lanes == GL)
    zeros = jnp.zeros((NB, 128), F32)
    while n >= 1:
        odd = eliminate([front[pl.ds(q * stride + step, n, stride=2 * step), :] for q in range(NB)])
        for q in range(NB):
            front[pl.ds(q * stride + step, n, stride=2 * step), :] = odd[q]
        plus = (zeros, zeros, zeros)
        for i in range(n):
            x = front[pl.ds((2 * i + 1) * step, NB, stride=stride), :]
            right = jnp.where((lanes >= NB) & (lanes < 2 * NB), x, 0.0)
            left = jnp.where(lanes >= LEFT, x, 0.0)
            rhs = jnp.where(lanes == GL, x, 0.0)
            minus = rhs + right + pltpu.roll(left, NB, 1)
            own = (split3f(minus), plus)
            plus = split3f(rhs + left + pltpu.roll(right, 128 - NB, 1))
            at = pl.ds(2 * i * step, NB, stride=stride)
            row = front[at, :]
            front[at, :] = jnp.where(near, row, 0.0) - meet(split3f(row), *own)
        levels.append((step, n))
        step, n = (2 * step, n // 2)

    last = eliminate([front[q * stride:q * stride + 1, :] for q in range(NB)])
    lanes = lane_iota(1)
    x0 = jnp.zeros((1, 128), F32)
    for q in range(NB):
        x0 = jnp.where(lanes == q, column(last[q], GL), x0)
    sol[8:9, :] = x0
    for step, n in reversed(levels):
        nxt = sol[pl.ds(8 + 2 * step, n, stride=2 * step), :]
        prv = sol[pl.ds(8, n, stride=2 * step), :]
        lanes = lane_iota(n)
        vec = pltpu.roll(nxt, NB, 1) + pltpu.roll(prv, LEFT, 1)
        vec = jnp.where(lanes == GL, -1.0, vec)
        x = jnp.zeros((n, 128), F32)
        for q in range(NB):
            row = front[pl.ds(q * stride + step, n, stride=2 * step), :]
            x = jnp.where(lanes == q, -jnp.sum(row * vec, axis=1, keepdims=True), x)
        sol[pl.ds(8 + step, n, stride=2 * step), :] = x
    out_ref[...] = -sol[8:8 + blocks, :]


def from_all(x, axis):
    size = lax.axis_size(axis)
    partner = lax.ppermute(x, axis, [(i, i ^ 1) for i in range(size)])
    pair = jnp.concatenate([x, partner], axis=0)
    parts = [pair]
    for k in range(2, size, 2):
        parts.append(lax.ppermute(pair, axis, [(i, i ^ k) for i in range(size)]))
    return parts


def sum_all(x, axis):
    size = lax.axis_size(axis)
    if size & (size - 1):
        return lax.psum(x, axis)
    parts = [x]
    for k in range(1, size):
        parts.append(lax.ppermute(x, axis, [(i, i ^ k) for i in range(size)]))
    while len(parts) > 1:
        parts = [parts[n] + parts[n + 1] for n in range(0, len(parts), 2)]
    return parts[0]


def beam_rows(beams):
    beam = np.arange(beams)
    rows = []
    for near in (beam, np.minimum(beam + 1, beams - 1), np.maximum(beam - 1, 0)):
        angle = np.float32(-0.4) + np.float32(0.7) * near.astype(np.float32) / np.float32(beams - 1)
        rows.append((np.cos(angle.astype(np.float64)), np.sin(angle.astype(np.float64))))
    (cos, sin), (cos_up, sin_up), (cos_dn, sin_dn) = rows
    return np.stack([cos, sin, cos_up, cos_dn, sin_up, sin_dn, cos, sin]).astype(np.float32)


def whole(shape):
    return pl.BlockSpec(shape, lambda r: (0,) * len(shape))


def local(
    ranges, valid_mask, match_tile, map_points, revolution_knot, spline_points, prior_weights
):
    revs, width, beams = ranges.shape
    knots = spline_points.shape[0]
    mapn = map_points.shape[0]
    blocks = knots // 4
    sectors = lax.axis_size("sector")
    sector = lax.axis_index("sector")
    total_revs = revs * lax.axis_size("rev")
    first = sector * width
    first_column = first.reshape(1).astype(jnp.int32)
    up = [(i, (i + 1) % sectors) for i in range(sectors)]
    down = [(j, i) for i, j in up]
    before = lax.ppermute(ranges[:, width - 1:, :], "sector", up)
    after = lax.ppermute(ranges[:, :1, :], "sector", down)

    rows = width + 2 * PAD
    column = (first - PAD + jnp.arange(rows, dtype=jnp.int32) + COLS) % COLS
    azimuth = 2.0 * jnp.pi * column.astype(F32) / COLS
    trig = jnp.stack([jnp.cos(azimuth), jnp.sin(azimuth)])
    trig = jnp.broadcast_to(trig[:, :, None], (2, rows, beams))
    beam_table = jnp.asarray(beam_rows(beams))

    smem = pl.BlockSpec(memory_space=pltpu.SMEM)
    per_rev = pl.BlockSpec((1, width, beams), lambda r: (r, 0, 0))
    edge = pl.BlockSpec((1, 1, beams), lambda r: (r, 0, 0))
    normal_spec = pl.BlockSpec((3, 1, width, beams), lambda r: (0, r, 0, 0))
    two_revs = pl.BlockSpec((2, width, beams), lambda r: (r, 0, 0))
    point_spec = pl.BlockSpec((3, 1, rows, beams), lambda r: (0, r, 0, 0))
    two_points = pl.BlockSpec((3, 2, rows, beams), lambda r: (0, r, 0, 0))
    two_normals = pl.BlockSpec((3, 2, width, beams), lambda r: (0, r, 0, 0))
    params = pltpu.CompilerParams(
        dimension_semantics=("arbitrary",), vmem_limit_bytes=56 * 1024 * 1024
    )
    normals, resid, sums, points = pl.pallas_call(
        functools.partial(points_kernel, width=width, mapn=mapn, revs=revs),
        grid=(revs,),
        in_specs=[
            smem, smem, smem, smem, per_rev, per_rev, edge, edge,
            whole((3, mapn, beams)), whole((2, rows, beams)), whole((8, beams)),
        ],
        out_specs=[normal_spec, per_rev, whole((8, beams)), point_spec],
        out_shape=[
            jax.ShapeDtypeStruct((3, revs, width, beams), F32),
            jax.ShapeDtypeStruct((revs, width, beams), F32),
            jax.ShapeDtypeStruct((8, beams), F32),
            jax.ShapeDtypeStruct((3, revs, rows, beams), F32),
        ],
        scratch_shapes=[
            pltpu.VMEM((mapn * 4 + 32, beams), F32),
            pltpu.VMEM((288, beams), F32),
            pltpu.VMEM((288, beams), F32),
        ],
        compiler_params=params,
        name="points",
    )(
        first_column, revolution_knot, spline_points.T, (match_tile * 4).reshape(-1),
        ranges, valid_mask, before, after, jnp.transpose(map_points, (1, 0, 2)), trig, beam_table,
    )
    sums = sum_all(sums, "sector")
    share = pl.pallas_call(
        functools.partial(gram_kernel, width=width, scale=1.0 / (COLS * beams), revs=revs),
        grid=(revs // 2,),
        in_specs=[
            smem, smem, two_points, two_revs, two_revs, two_normals, whole((8, beams)),
        ],
        out_specs=whole((4 * revs, beams)),
        out_shape=jax.ShapeDtypeStruct((4 * revs, beams), F32),
        scratch_shapes=[pltpu.VMEM((GRAD0, width, 128), BF16)] * 2
        + [
            pltpu.VMEM((8, 128), F32),
            pltpu.VMEM((16, 8, 128), F32),
            pltpu.VMEM((32, width), BF16),
        ],
        compiler_params=params,
        name="gram",
    )(first_column, revolution_knot, points, valid_mask, resid, normals, sums)
    share = sum_all(share, "sector")
    shares = from_all(share, "rev")
    own = lax.axis_index("rev").reshape(1).astype(jnp.int32)
    prior = jnp.pad(prior_weights.reshape(blocks, NB), ((0, 0), (0, beams - NB)))
    update = pl.pallas_call(
        functools.partial(
            solve_kernel, blocks=blocks, revs=total_revs, sources=len(shares)
        ),
        in_specs=[smem] + [pl.BlockSpec(memory_space=pltpu.VMEM)] * (len(shares) + 2),
        out_shape=jax.ShapeDtypeStruct((blocks, 128), F32),
        scratch_shapes=[
            pltpu.VMEM((4 * total_revs + 8, 128), F32),
            pltpu.VMEM(((NB + 2) * (blocks + 8), 128), F32),
            pltpu.VMEM((2 * blocks + 16, 128), F32),
        ],
        compiler_params=pltpu.CompilerParams(vmem_limit_bytes=40 * 1024 * 1024),
        name="solve",
    )(own, *shares, prior, jnp.asarray(PLACE, BF16))
    return (normals, update[:, :NB].reshape(knots * 6))


def solution(mesh):
    return jax.shard_map(
        local,
        mesh=mesh,
        in_specs=(
            P("rev", "sector", None),
            P("rev", "sector", None),
            P("rev", "sector"),
            P(),
            P("rev"),
            P(),
            P(),
        ),
        out_specs=(P(None, "rev", "sector", None), P()),
        check_vma=False,
    )
```
